256 devices in a mesh: space: 8 (over y, core), angle: 32 (over z, x).
Axes of the slice: x: 4, y: 4, z: 8, core: 2. Of those that a mesh axis runs over, the one named last changes fastest.
Arguments:
- image: float32 [32768, 128], P(('space', 'angle')), may hold values from 0 to 1
- tiles: bfloat16 [8, 3072, 128, 128], P('space', 'angle'), may hold values from -0.109375 to 0.109375
- tile_slot: int32 [8, 3072], P('space', 'angle'), may hold values from 0 to 7, as said below
- tile_block: int32 [8, 3072], P('space', 'angle'), may hold values from 0 to 31
- slot_ray: int32 [8, 256], P('space', 'angle'), may hold values from 0 to 31, as said below
- sinogram: bfloat16 [32, 32, 128, 128], P('angle', 'space'), may hold values from -4 to 4
- weights: bfloat16 [32, 32, 128, 128], P('angle', 'space'), may hold values from 0.29882812 to 3
Outputs:
- volume: float32 [32768, 128], P(('space', 'angle'))
- residual: bfloat16 [32, 32, 128, 128], P('angle', 'space')
The draws below stay inside these ranges and needn't reach their ends.
Inputs may be any that keep to these rules, and one draw needn't show every extreme that they name: `tile_slot`: every slot of a device is fed by at least one of its tiles. `slot_ray`: the 8 entries of one device are distinct; of the ray blocks k * 4 to (k + 1) * 4 - 1 of its angle group, one device lists at most 2, and in every angle group some k is listed 2 times by every device of the group.
All inputs are finite; a program needn't handle non-finite values.
Results may differ from the reference program's by a relative error of at most 0.025.
Values may be sent and summed in bfloat16 or wider, within the bound.
No kernel may reach another device: no remote copies, remote signals or barrier semaphores. Data moves between devices by JAX's collectives and lax.ppermute only.
A program may use at most 64 MiB of HBM per device.

```python
import math
import jax
import jax.numpy as jnp
from jax import lax

TILE = 128
SLICES = 128
TILES_DEV = 96
BLOCKS = 32
SLOTS = 8
CAP = 2
OWN = 4
ITERS = 2
RAYS = 32
IMAGE_ROWS = 32768
N_SPACE = 8
N_ANGLE = 32


def draw_tile_slot(key, part):

    def per_device(device):
        ordering = jax.random.permutation(jax.random.fold_in(key, device + 3), TILES_DEV)
        return (ordering % SLOTS).astype(jnp.int32)
    listed = jax.vmap(per_device)(jnp.arange(N_SPACE * N_ANGLE, dtype=jnp.int32))
    return listed.reshape(N_SPACE, N_ANGLE * TILES_DEV)


def draw_slot_ray(key, part):
    hot_owner = jax.random.randint(jax.random.fold_in(key, 7), (N_ANGLE,), 0, N_SPACE)

    def per_device(device):
        angle_group = device % N_ANGLE
        device_key = jax.random.fold_in(key, device + 11)
        first_key, second_key, third_key = jax.random.split(device_key, 3)
        seat_order = jax.random.permutation(first_key, (N_SPACE - 1) * CAP)[:SLOTS - CAP]
        other_owner = seat_order // CAP
        counts_other = jnp.sum((other_owner[:, None] == jnp.arange(N_SPACE - 1)[None, :]).astype(jnp.int32), axis=0)
        owners = jnp.arange(N_SPACE)
        hot_here = hot_owner[angle_group]
        shifted = jnp.clip(owners - (owners > hot_here).astype(jnp.int32), 0, N_SPACE - 2)
        counts = jnp.where(owners == hot_here, CAP, counts_other[shifted])
        owner_keys = jax.random.split(second_key, N_SPACE)

        def choose(owner_key):
            return jax.random.permutation(owner_key, OWN)[:CAP]
        chosen = jax.vmap(choose)(owner_keys)
        seat_rank = jnp.arange(CAP)
        is_live = seat_rank[None, :] < counts[:, None]
        ray_list = owners[:, None] * OWN + chosen
        sort_keys = jnp.where(is_live, owners[:, None] * CAP + seat_rank[None, :], N_SPACE * CAP + 1)
        ordering = jnp.argsort(sort_keys.reshape(-1), stable=True)[:SLOTS]
        picked = ray_list.reshape(-1)[ordering]
        shuffle = jax.random.permutation(third_key, SLOTS)
        return picked[shuffle].astype(jnp.int32)
    listed = jax.vmap(per_device)(jnp.arange(N_SPACE * N_ANGLE, dtype=jnp.int32))
    return listed.reshape(N_SPACE, N_ANGLE * SLOTS)


def set_ends(result, stream_key, least, top_value):
    index_at = [jax.random.randint(jax.random.fold_in(stream_key, axis), (), 0, length) for axis, length in enumerate(result.shape)]
    longest = result.shape.index(max(result.shape))
    next_to = index_at[:longest] + [(index_at[longest] + 1) % result.shape[longest]] + index_at[longest + 1:]
    return result.at[tuple(index_at)].set(least).at[tuple(next_to)].set(top_value)


def block_scale(rng, extent, cuts, low, largest):
    factor_of = 1.0
    for position, parts in cuts:
        draws = jax.random.uniform(jax.random.fold_in(jax.random.fold_in(rng, 6), position), (parts,), jnp.float32, low / len(cuts), largest / len(cuts))
        factor_of = factor_of * jnp.repeat(jnp.exp(draws), extent[position] // parts).reshape((-1,) + (1,) * (len(extent) - 1 - position))
    return factor_of


def noise(rng, extent, deviation, reach, pieces=(), kind=jnp.bfloat16):
    factor_of = block_scale(rng, extent, pieces, -0.22, 0.18) if pieces else 1.0
    drawn = jax.random.normal(rng, extent, jnp.float32) * deviation * factor_of
    return jnp.minimum(jnp.maximum(drawn, -reach), reach).astype(kind)


def setup_inputs(seed: int = 0) -> dict:
    key_of = jax.random.split(jax.random.key(seed), 8)
    return {
        "image": jnp.clip(1.0 * jax.random.uniform(key_of[0], (IMAGE_ROWS, SLICES), jnp.float32) ** block_scale(key_of[0], (IMAGE_ROWS, SLICES), ((0, 256),), -0.2, 0.2), 0.0, 1.0),
        "tiles": noise(key_of[1], (N_SPACE, N_ANGLE * TILES_DEV, TILE, TILE), (TILE * TILES_DEV * N_SPACE // RAYS) ** -0.5, 0.109375, ((0, 8), (1, 32))),
        "tile_slot": draw_tile_slot(jax.random.fold_in(key_of[7], 71), 0),
        "tile_block": set_ends(jax.random.randint(key_of[3], (N_SPACE, N_ANGLE * TILES_DEV), 0, BLOCKS), jax.random.fold_in(key_of[3], 1), 0, BLOCKS - 1).astype(jnp.int32),
        "slot_ray": draw_slot_ray(jax.random.fold_in(key_of[7], 71), 0),
        "sinogram": noise(key_of[5], (N_ANGLE, RAYS, TILE, SLICES), 0.6, 4.0, ((0, 32), (1, 8))),
        "weights": jnp.clip(jnp.exp(math.log(3.0) - 2.306499 * jax.random.uniform(key_of[6], (N_ANGLE, RAYS, TILE, SLICES), jnp.float32) ** block_scale(key_of[6], (N_ANGLE, RAYS, TILE, SLICES), ((0, 32), (1, 8)), -0.2, 0.2)), 0.29882812, 3.0).astype(jnp.bfloat16),
    }


def reference(image, tiles, tile_slot, tile_block, slot_ray, sinogram, weights):
    tile_sets = tiles.reshape(N_SPACE, N_ANGLE, TILES_DEV, TILE, TILE)
    slot_sets = tile_slot.reshape(N_SPACE, N_ANGLE, TILES_DEV).astype(jnp.int32)
    block_sets = tile_block.reshape(N_SPACE, N_ANGLE, TILES_DEV).astype(jnp.int32)
    ray_sets = slot_ray.reshape(N_SPACE, N_ANGLE, SLOTS).astype(jnp.int32)
    step_size = 0.2 * math.sqrt(BLOCKS / (N_ANGLE * OWN))
    observed = sinogram.astype(jnp.float32)
    scales = weights.astype(jnp.float32)
    spaces = jnp.arange(N_SPACE, dtype=jnp.int32)
    angles = jnp.arange(N_ANGLE, dtype=jnp.int32)
    current = image
    residual = None
    for iteration in range(ITERS):
        pixels = current.astype(jnp.bfloat16).reshape(N_SPACE, BLOCKS, TILE, SLICES)

        def project(angle_group):

            def add_domain(running, space_index):
                tile_mats = tile_sets[space_index, angle_group].astype(jnp.float32)
                picked = pixels[space_index][block_sets[space_index, angle_group]].astype(jnp.float32)
                products = jnp.einsum('tij,tjk->tik', tile_mats, picked)
                partial_value = jax.ops.segment_sum(products, slot_sets[space_index, angle_group], num_segments=SLOTS)
                partial_value = lax.optimization_barrier(partial_value.astype(jnp.bfloat16)).astype(jnp.float32)
                running = running.at[ray_sets[space_index, angle_group]].add(partial_value)
                return (running, None)
            running, _ = lax.scan(add_domain, jnp.zeros((RAYS, TILE, SLICES), jnp.float32), spaces)
            return running
        ray_sums = lax.map(project, angles)
        residual = (scales * (ray_sums - observed)).astype(jnp.bfloat16)

        def backproject(space_index):

            def add_angle(running, angle_group):
                tile_mats = tile_sets[space_index, angle_group].astype(jnp.float32)
                slot_res = residual[angle_group][ray_sets[space_index, angle_group]]
                tile_res = slot_res[slot_sets[space_index, angle_group]].astype(jnp.float32)
                back_terms = jnp.einsum('tji,tjk->tik', tile_mats, tile_res)
                block_part = jax.ops.segment_sum(back_terms, block_sets[space_index, angle_group], num_segments=BLOCKS)
                block_part = lax.optimization_barrier(block_part.astype(jnp.bfloat16)).astype(jnp.float32)
                return (running + block_part, None)
            running, _ = lax.scan(add_angle, jnp.zeros((BLOCKS, TILE, SLICES), jnp.float32), angles)
            return running
        gradient = lax.map(backproject, spaces).reshape(N_SPACE * BLOCKS * TILE, SLICES)
        current = jnp.maximum(current - step_size * gradient, 0.0)
    return (current, residual)
```

```python
import functools
import math

import jax
import jax.numpy as jnp
from jax import lax
from jax.experimental import pallas as pl
from jax.experimental.pallas import tpu as pltpu
from jax.sharding import PartitionSpec as P

ITERS = 2
CAP = 2
NX = 4
META = 16
UNROLL = 8

SMEM = pl.BlockSpec(memory_space=pltpu.SMEM)
VMEM = pl.BlockSpec(memory_space=pltpu.VMEM)


def params(mib):
    return pltpu.CompilerParams(vmem_limit_bytes=mib << 20)


def place_slots(ray_ref, pos_ref, idx_ref, own):
    slots = ray_ref.shape[0]
    for seat in range(idx_ref.shape[0]):
        idx_ref[seat] = -1
    rays = [ray_ref[j] for j in range(slots)]
    owners = [r // own for r in rays]
    for j in range(slots):
        rank = jnp.int32(0)
        for i in range(j):
            rank += (owners[i] == owners[j]).astype(jnp.int32)
        seat = owners[j] * CAP + jnp.minimum(rank, CAP - 1)
        pos_ref[j] = seat
        idx_ref[seat] = rays[j] - owners[j] * own


def block_seat(b, nz):
    return (b % NX) * nz + b // NX


def forward_kernel(own, slot_ref, block_ref, ray_ref, tiles_ref, pix_ref, out_ref, acc, pos, idx):
    nz = pix_ref.shape[0] // NX
    tiles, edge, _ = tiles_ref.shape
    place_slots(ray_ref, pos, idx, own)
    acc[...] = jnp.zeros_like(acc)
    out_ref[...] = jnp.zeros_like(out_ref)

    def step(i, carry):
        for u in range(UNROLL):
            t = i * UNROLL + u
            j = slot_ref[t]
            p = block_seat(block_ref[t], nz)
            acc[j] += jnp.dot(tiles_ref[t], pix_ref[p], preferred_element_type=jnp.float32)
        return carry

    lax.fori_loop(0, tiles // UNROLL, step, 0)
    for j in range(acc.shape[0]):
        seat = pos[j]
        out_ref[seat // CAP, pl.ds(pl.multiple_of((seat % CAP) * edge, edge), edge), :] = acc[j].astype(
            jnp.bfloat16
        )
    if out_ref.shape[1] > CAP * edge:
        row = lax.broadcasted_iota(jnp.int32, (META, out_ref.shape[2]), 0)
        for k in range(out_ref.shape[0]):
            value = jnp.where(row < META // CAP, idx[k * CAP], idx[k * CAP + 1])
            out_ref[k, pl.ds(CAP * edge, META), :] = value.astype(jnp.float32).astype(jnp.bfloat16)


def owner_kernel(recv_ref, meta_ref, obs_ref, scale_ref, res_ref, back_ref):
    spaces = recv_ref.shape[0]
    own, edge, slices = obs_ref.shape
    step = 16
    seats = [(s, r) for s in range(spaces) for r in range(CAP)]
    marks = {}
    for s in range(spaces):
        value = meta_ref[s].astype(jnp.float32)
        for r in range(CAP):
            marks[s, r] = value[r * (META // CAP) : r * (META // CAP) + 1, :]
    for c in range(edge // step):
        sums = [jnp.zeros((step, slices), jnp.float32) for _ in range(own)]
        for s, r in seats:
            data = recv_ref[s, r * edge + c * step : r * edge + (c + 1) * step, :].astype(jnp.float32)
            mark = jnp.broadcast_to(marks[s, r], (step, slices))
            for o in range(own):
                sums[o] += jnp.where(mark == float(o), data, 0.0)
        rows = slice(c * step, (c + 1) * step)
        for o in range(own):
            obs = obs_ref[o, rows, :].astype(jnp.float32)
            scale = scale_ref[o, rows, :].astype(jnp.float32)
            res_ref[o, rows, :] = (scale * (sums[o] - obs)).astype(jnp.bfloat16)
    flipped = [res_ref[o].astype(jnp.float32).T for o in range(own)]
    for s, r in seats:
        mark = jnp.broadcast_to(marks[s, r], (edge, slices))
        value = flipped[own - 1]
        for o in range(own - 1):
            value = jnp.where(mark == float(o), flipped[o], value)
        back_ref[s, r * edge : (r + 1) * edge, :] = value.astype(jnp.bfloat16)


def backward_kernel(own, slot_ref, block_ref, ray_ref, tiles_ref, res_ref, out_ref, acc, pos, idx):
    nz = out_ref.shape[0] // NX
    tiles = tiles_ref.shape[0]
    place_slots(ray_ref, pos, idx, own)
    acc[...] = jnp.zeros_like(acc)

    def step(i, carry):
        for u in range(UNROLL):
            t = i * UNROLL + u
            seat = pos[slot_ref[t]]
            p = block_seat(block_ref[t], nz)
            acc[p] += jnp.dot(res_ref[seat], tiles_ref[t], preferred_element_type=jnp.float32)
        return carry

    lax.fori_loop(0, tiles // UNROLL, step, 0)
    out_ref[...] = acc[...].astype(jnp.bfloat16)


def update_kernel(step_size, grad_ref, cur_ref, new_ref, *copies):
    total = grad_ref[0].astype(jnp.float32)
    for k in range(1, grad_ref.shape[0]):
        total += grad_ref[k].astype(jnp.float32)
    new = jnp.maximum(cur_ref[...] - step_size * total.T, 0.0)
    new_ref[...] = new
    for copy in copies:
        value = new.astype(jnp.bfloat16)
        for k in range(copy.shape[0]):
            copy[k] = value


def shards(image, tiles, tile_slot, tile_block, slot_ray, sinogram, weights):
    n_space = lax.axis_size("space")
    n_angle = lax.axis_size("angle")
    nz = n_angle // NX
    x_groups = [[z * NX + x for x in range(NX)] for z in range(nz)]
    z_groups = [[z * NX + x for z in range(nz)] for x in range(NX)]
    tile_mats = tiles[0]
    own = sinogram.shape[1]
    edge = tile_mats.shape[1]
    slices = image.shape[1]
    blocks = image.shape[0] * n_angle // edge
    slots = slot_ray.shape[1]
    step_size = 0.2 * math.sqrt(blocks / (n_angle * own))
    obs, scale = sinogram[0], weights[0]
    lists = (tile_slot[0], tile_block[0], slot_ray[0])
    bf16, f32 = jnp.bfloat16, jnp.float32
    seats = pltpu.SMEM((slots,), jnp.int32), pltpu.SMEM((n_space * CAP,), jnp.int32)

    def to_all(x, axis, groups=None):
        return lax.all_to_all(x, axis, 0, 0, axis_index_groups=groups, tiled=True)

    def gather(copies):
        column = to_all(copies, "angle", z_groups)
        wide = jnp.broadcast_to(column[None], (NX, nz, edge, slices)).reshape(blocks, edge, slices)
        return to_all(wide, "angle", x_groups)

    current = image
    pixels = gather(jnp.broadcast_to(image.astype(bf16)[None], (nz, edge, slices)))
    meta = None
    for iteration in range(ITERS):
        rows = CAP * edge + (META if iteration == 0 else 0)
        sent = pl.pallas_call(
            functools.partial(forward_kernel, own),
            out_shape=jax.ShapeDtypeStruct((n_space, rows, slices), bf16),
            in_specs=[SMEM] * 3 + [VMEM] * 2,
            out_specs=VMEM,
            scratch_shapes=[pltpu.VMEM((slots, edge, slices), f32), *seats],
            compiler_params=params(12),
            name="forward",
        )(*lists, tile_mats, pixels)
        recv = to_all(sent, "space")
        if iteration == 0:
            meta = recv[:, CAP * edge :, :]
        residual, back = pl.pallas_call(
            owner_kernel,
            out_shape=(
                jax.ShapeDtypeStruct((own, edge, slices), bf16),
                jax.ShapeDtypeStruct((n_space, CAP * edge, slices), bf16),
            ),
            in_specs=[VMEM] * 4,
            out_specs=(VMEM, VMEM),
            compiler_params=params(12),
            name="owner",
        )(recv, meta, obs, scale)
        slot_res = to_all(back, "space").reshape(n_space * CAP, slices, edge)
        grad_part = pl.pallas_call(
            functools.partial(backward_kernel, own),
            out_shape=jax.ShapeDtypeStruct((blocks, slices, edge), bf16),
            in_specs=[SMEM] * 3 + [VMEM] * 2,
            out_specs=VMEM,
            scratch_shapes=[pltpu.VMEM((blocks, slices, edge), f32), *seats],
            compiler_params=params(16),
            name="backward",
        )(*lists, tile_mats, slot_res)
        across = to_all(grad_part, "angle", x_groups).reshape(NX, nz, slices, edge)
        column = jnp.sum(across.astype(f32), axis=0).astype(bf16)
        terms = to_all(column, "angle", z_groups)
        more = iteration + 1 < ITERS
        shapes = [jax.ShapeDtypeStruct((edge, slices), f32)]
        if more:
            shapes.append(jax.ShapeDtypeStruct((nz, edge, slices), bf16))
        current, *copies = pl.pallas_call(
            functools.partial(update_kernel, step_size),
            out_shape=tuple(shapes),
            in_specs=[VMEM] * 2,
            out_specs=(VMEM,) * len(shapes),
            compiler_params=params(8),
            name="update",
        )(terms, current)
        if more:
            pixels = gather(copies[0])
    return (current, residual[None])


def solution(mesh):
    placed = (
        P(("space", "angle"), None),
        P("space", "angle", None, None),
        P("space", "angle"),
        P("space", "angle"),
        P("space", "angle"),
        P("angle", "space", None, None),
        P("angle", "space", None, None),
    )
    return jax.shard_map(
        shards,
        mesh=mesh,
        in_specs=placed,
        out_specs=(P(("space", "angle"), None), P("angle", "space", None, None)),
        check_vma=False,
    )
```

```python
import functools
import math

import jax
import jax.numpy as jnp
from jax import lax
from jax.experimental import pallas as pl
from jax.experimental.pallas import tpu as pltpu
from jax.sharding import PartitionSpec as P

ITERS = 2
NX = 4
CORES = 2
UNROLL = 8
SIDES, ACROSS = (1, 3), 2

SMEM = pl.BlockSpec(memory_space=pltpu.SMEM)
VMEM = pl.BlockSpec(memory_space=pltpu.VMEM)
BF16, F32 = jnp.bfloat16, jnp.float32

ROOM = 128
TILE, SLOT, ROW, START, STEPS, SEND, TAKE, TABLE = 0, ROOM, 2 * ROOM, 384, 392, 400, 416, 512


def group_of(block, me):
    return lax.rem(lax.rem(block, NX) - me + NX, NX)


def table_kernel(own, ny, nz, slot_ref, block_ref, ray_ref, tab):
    tiles, slots = slot_ref.shape[0], ray_ref.shape[0]
    here, me = lax.axis_index("space"), lax.rem(lax.axis_index("angle"), NX)
    y, core = here // CORES, lax.rem(here, CORES)
    zero = jnp.int32(0)

    def clear(i, carry):
        for u in range(UNROLL):
            tab[TILE + i * UNROLL + u] = zero
            tab[SLOT + i * UNROLL + u] = jnp.int32(slots)
            tab[ROW + i * UNROLL + u] = jnp.int32(nz)
        return carry

    lax.fori_loop(0, ROOM // UNROLL, clear, 0)

    def count(i, counts):
        for u in range(4):
            d = group_of(block_ref[i * 4 + u], me)
            counts = tuple(c + (d == g).astype(jnp.int32) for g, c in enumerate(counts))
        return counts

    counts = lax.fori_loop(0, tiles // 4, count, (zero,) * NX)
    starts, at = [], zero
    for g in range(NX):
        steps = (counts[g] + UNROLL - 1) // UNROLL
        starts.append(at)
        tab[START + g] = at
        tab[STEPS + g] = steps
        at = at + steps * UNROLL

    def place(i, cursors):
        for u in range(4):
            t = i * 4 + u
            b = block_ref[t]
            d = group_of(b, me)
            seat = cursors[0]
            for g in range(1, NX):
                seat = jnp.where(d == g, cursors[g], seat)
            tab[TILE + seat] = t
            tab[SLOT + seat] = slot_ref[t]
            tab[ROW + seat] = b // NX
            cursors = tuple(c + (d == g).astype(jnp.int32) for g, c in enumerate(cursors))
        return cursors

    lax.fori_loop(0, tiles // 4, place, tuple(starts))
    for j in range(slots):
        ray = ray_ref[j]
        owner = ray // own
        o = ray - owner * own
        theirs = owner // CORES
        side = jnp.where(lax.rem(owner, CORES) == core, 0, ny)
        tab[SEND + j] = (side + lax.rem(theirs - y + ny, ny)) * own + o
        tab[TAKE + j] = (side + lax.rem(y - theirs + ny, ny)) * own + o


def sweep(tab, group, body):
    start = tab[START + group]

    def step(i, carry):
        for u in range(UNROLL):
            at = start + i * UNROLL + u
            body(tab[TILE + at], tab[SLOT + at], tab[ROW + at])
        return carry

    lax.fori_loop(0, tab[STEPS + group], step, 0)


def forward_kernel(groups, first, last, tab, tiles_ref, *refs):
    columns, refs = refs[: len(groups)], refs[len(groups) :]
    before, outs, acc = refs[: 1 - first], refs[1 - first : -1], refs[-1]
    slots = acc.shape[0] - 1
    if first:
        acc[...] = jnp.zeros_like(acc)
    else:
        acc[:slots] = before[0][...]
        acc[slots] = jnp.zeros_like(acc[slots])
    for group, column in zip(groups, columns):

        def body(t, j, z):
            pixels = column[jnp.minimum(z, column.shape[0] - 1)]
            acc[j] += jnp.dot(tiles_ref[t], pixels, preferred_element_type=F32)

        sweep(tab, group, body)
    if not last:
        outs[0][...] = acc[:slots]
        return
    half = outs[0].shape[0]
    for out in outs:
        out[...] = jnp.zeros_like(out)
    for j in range(slots):
        seat = tab[SEND + j]

        @pl.when(seat < half)
        def _():
            outs[0][seat] = acc[j].astype(BF16)

        @pl.when(seat >= half)
        def _():
            outs[1][seat - half] = acc[j].astype(BF16)


def merge_kernel(own, mine_ref, other_ref, near_ref, *far_refs):
    near_ref[...] = mine_ref[:own].astype(F32) + other_ref[:own].astype(F32)
    for d, ref in enumerate(far_refs, 1):
        rows = slice(d * own, (d + 1) * own)
        ref[...] = (mine_ref[rows].astype(F32) + other_ref[rows].astype(F32)).astype(BF16)


def owner_kernel(obs_ref, scale_ref, near_ref, *refs):
    far, (res_ref, flip_ref) = refs[:-2], refs[-2:]
    for o in range(obs_ref.shape[0]):
        total = near_ref[o]
        for ref in far:
            total += ref[o].astype(F32)
        value = scale_ref[o].astype(F32) * (total - obs_ref[o].astype(F32))
        res_ref[o] = value.astype(BF16)
        flip_ref[o] = value.T.astype(BF16)


def backward_kernel(groups, first, tab, tiles_ref, *refs):
    acc = refs[-1]
    if first:
        rays = refs[-2]
        ins, outs, mine_ref = refs[: -3 - len(groups)], refs[-3 - len(groups) : -3], refs[-3]
        own = ins[0].shape[0]
        for n, ref in enumerate(ins):
            rays[n * own : (n + 1) * own] = ref[...]
        for j in range(mine_ref.shape[0]):
            mine_ref[j] = rays[tab[TAKE + j]]
    else:
        mine_ref, outs = refs[0], refs[1:-1]
    slots, nz = mine_ref.shape[0], outs[0].shape[0]
    for group, out in zip(groups, outs):
        acc[...] = jnp.zeros_like(acc)

        def body(t, j, z):
            rays = mine_ref[jnp.minimum(j, slots - 1)]
            acc[z] += jnp.dot(rays, tiles_ref[t], preferred_element_type=F32)

        sweep(tab, group, body)
        out[...] = acc[:nz].astype(BF16)


def sum_kernel(*refs):
    total = refs[0][...].astype(F32)
    for ref in refs[1:-1]:
        total += ref[...].astype(F32)
    refs[-1][...] = total.astype(BF16)


def update_kernel(step_size, grad_ref, cur_ref, new_ref, *copies):
    total = grad_ref[0].astype(F32)
    for k in range(1, grad_ref.shape[0]):
        total += grad_ref[k].astype(F32)
    new = jnp.maximum(cur_ref[...] - step_size * total.T, 0.0)
    new_ref[...] = new
    for copy in copies:
        value = new.astype(BF16)
        for k in range(copy.shape[0]):
            copy[k] = value


def call(kernel, shapes, specs, mib, scratch=(), out=VMEM, work=0):
    return pl.pallas_call(
        kernel,
        out_shape=tuple(jax.ShapeDtypeStruct(shape, dtype) for shape, dtype in shapes),
        in_specs=specs,
        out_specs=(out,) * len(shapes),
        scratch_shapes=list(scratch),
        compiler_params=pltpu.CompilerParams(vmem_limit_bytes=mib << 20),
        cost_estimate=pl.CostEstimate(flops=work, transcendentals=0, bytes_accessed=2 << 20),
    )


def shards(image, tiles, tile_slot, tile_block, slot_ray, sinogram, weights):
    n_space = lax.axis_size("space")
    n_angle = lax.axis_size("angle")
    nz, ny = n_angle // NX, n_space // CORES
    z_groups = [[z * NX + x for z in range(nz)] for x in range(NX)]
    tile_mats = tiles[0]
    own = sinogram.shape[1]
    edge = tile_mats.shape[1]
    slices = image.shape[1]
    blocks = image.shape[0] * n_angle // edge
    slots = slot_ray.shape[1]
    count = tile_slot.shape[1]
    step_size = 0.2 * math.sqrt(blocks / (n_angle * own))
    tile = (edge, slices)
    quarter = 2 * edge * edge * slices * count // NX
    sums = pltpu.VMEM((slots + 1, *tile), F32)
    block_sums = pltpu.VMEM((nz + 1, *tile), F32)

    def along_x(value, d):
        return lax.ppermute(value, "angle", [(i, i // NX * NX + (i + d) % NX) for i in range(n_angle)])

    def along_y(value, d):
        return lax.ppermute(value, "space", [(i, (i + d * CORES) % n_space) for i in range(n_space)])

    def across(value):
        return lax.ppermute(value, "space", [(i, i ^ 1) for i in range(n_space)])

    def along_z(value):
        return lax.all_to_all(value, "angle", 0, 0, axis_index_groups=z_groups, tiled=True)

    def iterate(iteration, current, copies, table):
        column = along_z(copies)
        if table is None:
            (table,) = call(
                functools.partial(table_kernel, own, ny, nz),
                [((TABLE,), jnp.int32)],
                [SMEM] * 3,
                4,
                out=SMEM,
                work=quarter,
            )(tile_slot[0], tile_block[0], slot_ray[0])
        lists = (table, tile_mats)
        columns = {d: along_x(column, d) for d in (*SIDES, ACROSS)}

        def project(distances, before=None):
            first, last = before is None, ACROSS in distances
            received = [column if d == 0 else columns[d] for d in distances]
            return call(
                functools.partial(forward_kernel, [(NX - d) % NX for d in distances], first, last),
                [((ny * own, *tile), BF16)] * 2 if last else [((slots, *tile), F32)],
                [SMEM] + [VMEM] * (1 + len(distances) + (not first)),
                12,
                [sums],
                work=quarter * len(distances),
            )(*lists, *received, *(() if first else (before,)))

        (partial,) = project((0,))
        (partial,) = project(SIDES, partial)
        mine, other = project((ACROSS,), partial)
        near, *far = call(
            functools.partial(merge_kernel, own),
            [((own, *tile), F32)] + [((own, *tile), BF16)] * (ny - 1),
            [VMEM] * 2,
            8,
        )(mine, across(other))
        residual, flipped = call(
            owner_kernel, [((own, *tile), BF16)] * 2, [VMEM] * (2 + ny), 8
        )(sinogram[0], weights[0], near, *[along_y(far[d - 1], d) for d in range(1, ny)])
        same = [flipped] + [along_y(flipped, d) for d in range(1, ny)]
        rays = same + [across(value) for value in same]

        def backproject(groups, operands, first):
            return call(
                functools.partial(backward_kernel, groups, first),
                [((nz, *tile), BF16)] * len(groups) + [((slots, *tile), BF16)] * first,
                [SMEM] + [VMEM] * (1 + len(operands)),
                12,
                [pltpu.VMEM((n_space * own, *tile), BF16)] * first + [block_sums],
                work=quarter * len(groups),
            )(*lists, *operands)

        *parts, slot_res = backproject(SIDES, rays, True)
        summed = [along_x(part, d) for d, part in zip(SIDES, parts)]
        (part,) = backproject((ACROSS,), [slot_res], False)
        summed.append(along_x(part, ACROSS))
        (part,) = backproject((0,), [slot_res], False)
        (column,) = call(sum_kernel, [((nz, *tile), BF16)], [VMEM] * NX, 8)(part, *summed)
        terms = along_z(column)
        more = iteration + 1 < ITERS
        current, *rest = call(
            functools.partial(update_kernel, step_size),
            [(tile, F32)] + [((nz, *tile), BF16)] * more,
            [VMEM] * 2,
            8,
        )(terms, current)
        return (current, residual, rest[0] if more else None, table)

    current, table = image, None
    copies = jnp.broadcast_to(image.astype(BF16)[None], (nz, *tile))
    for iteration in range(ITERS):
        current, residual, copies, table = iterate(iteration, current, copies, table)
    return (current, residual[None])


def solution(mesh):
    placed = (
        P(("space", "angle"), None),
        P("space", "angle", None, None),
        P("space", "angle"),
        P("space", "angle"),
        P("space", "angle"),
        P("angle", "space", None, None),
        P("angle", "space", None, None),
    )
    return jax.shard_map(
        shards,
        mesh=mesh,
        in_specs=placed,
        out_specs=(P(("space", "angle"), None), P("angle", "space", None, None)),
        check_vma=False,
    )
```

```python
import functools
import math

import jax
import jax.numpy as jnp
from jax import lax
from jax.experimental import pallas as pl
from jax.experimental.pallas import tpu as pltpu
from jax.sharding import PartitionSpec as P

ITERS = 2
NX = 4
CORES = 2
UNROLL = 26
RIGHT, ACROSS, LEFT = 1, 2, 3

SMEM = pl.BlockSpec(memory_space=pltpu.SMEM)
VMEM = pl.BlockSpec(memory_space=pltpu.VMEM)
HBM = pl.BlockSpec(memory_space=pltpu.HBM)
BF16, F32 = jnp.bfloat16, jnp.float32

ROOM = 128
TILE, SEAT, SLOT, SEND, TAKE, STEPS, TABLE = 0, ROOM, 2 * ROOM, 320, 336, 352, 384


def table_kernel(own, ny, nz, *refs):
    sources, (tab, near_tiles), lists, sems = refs[:4], refs[4:6], refs[6:9], refs[9]
    slot_ref, block_ref, ray_ref = lists
    tiles, slots = slot_ref.shape[0], ray_ref.shape[0]
    targets = (*lists, near_tiles.at[pl.ds(0, tiles)])
    copies = [
        pltpu.make_async_copy(source, target, sems.at[n]) for n, (source, target) in enumerate(zip(sources, targets))
    ]
    for copy in copies:
        copy.start()
    near_tiles[tiles] = jnp.zeros_like(near_tiles[tiles])
    here, me = lax.axis_index("space"), lax.rem(lax.axis_index("angle"), NX)
    y, core = here // CORES, lax.rem(here, CORES)
    zero = jnp.int32(0)

    def clear(i, carry):
        for u in range(8):
            tab[TILE + i * 8 + u] = jnp.int32(tiles)
            tab[SEAT + i * 8 + u] = zero
        for u in range(4):
            tab[SLOT + i * 4 + u] = zero
        return carry

    lax.fori_loop(0, ROOM // 8, clear, 0)
    for copy in copies[:3]:
        copy.wait()

    def count(i, counts):
        for u in range(4):
            j = slot_ref[i * 4 + u]
            counts = tuple(c + (j == g).astype(jnp.int32) for g, c in enumerate(counts))
        return counts

    counts = lax.fori_loop(0, tiles // 4, count, (zero,) * slots)
    at = zero
    for j in range(slots):
        ray = ray_ref[j]
        owner = ray // own
        o = ray - owner * own
        theirs = owner // CORES
        side = jnp.where(lax.rem(owner, CORES) == core, 0, ny)
        tab[SEND + j] = (side + lax.rem(theirs - y + ny, ny)) * own + o
        tab[TAKE + j] = (side + lax.rem(y - theirs + ny, ny)) * own + o
        ray_ref[j] = at
        pairs = (counts[j] + 1) // 2

        def mark(i, carry, j=j, first=at // 2):
            tab[SLOT + first + i] = jnp.int32(j)
            return carry

        lax.fori_loop(0, pairs, mark, 0)
        at = at + 2 * pairs
    tab[STEPS] = (at + 2 * UNROLL - 1) // (2 * UNROLL)

    def place(i, carry):
        for u in range(4):
            t = i * 4 + u
            b, j = block_ref[t], slot_ref[t]
            seat = ray_ref[j]
            ray_ref[j] = seat + 1
            tab[TILE + seat] = t
            tab[SEAT + seat] = lax.rem(me - lax.rem(b, NX) + NX, NX) * nz + b // NX
        return carry

    lax.fori_loop(0, tiles // 4, place, 0)
    copies[3].wait()


def sweep(tab, body):
    def step(i, carry):
        for u in range(UNROLL):
            pair = i * UNROLL + u
            body(tab[SLOT + pair], *[tab[at + 2 * pair + n] for at in (TILE, SEAT) for n in (0, 1)])
        return carry

    lax.fori_loop(0, tab[STEPS], step, 0)


def forward_kernel(tab, tiles_ref, *refs):
    columns, (mine_ref, other_ref, acc, pix) = refs[:NX], refs[NX:]
    nz, half = columns[0].shape[0], mine_ref.shape[0]
    for d, column in enumerate(columns):
        pix[d * nz : (d + 1) * nz] = column[...]
    acc[...] = jnp.zeros_like(acc)
    for out in (mine_ref, other_ref):
        out[...] = jnp.zeros_like(out)

    def body(j, t, u, p, q):
        pair = jnp.concatenate([tiles_ref[t], tiles_ref[u]], axis=1)
        pixels = jnp.concatenate([pix[p], pix[q]], axis=0)
        acc[j] += jnp.dot(pair, pixels, preferred_element_type=F32)

    sweep(tab, body)
    for j in range(acc.shape[0]):
        seat = tab[SEND + j]

        @pl.when(seat < half)
        def _():
            mine_ref[seat] = acc[j].astype(BF16)

        @pl.when(seat >= half)
        def _():
            other_ref[seat - half] = acc[j].astype(BF16)


def merge_kernel(own, mine_ref, other_ref, near_ref, *far_refs):
    near_ref[...] = mine_ref[:own].astype(F32) + other_ref[:own].astype(F32)
    for d, ref in enumerate(far_refs, 1):
        rows = slice(d * own, (d + 1) * own)
        ref[...] = (mine_ref[rows].astype(F32) + other_ref[rows].astype(F32)).astype(BF16)


def owner_kernel(obs_ref, scale_ref, near_ref, *refs):
    far, (res_ref, flip_ref) = refs[:-2], refs[-2:]
    for o in range(obs_ref.shape[0]):
        total = near_ref[o]
        for ref in far:
            total += ref[o].astype(F32)
        value = scale_ref[o].astype(F32) * (total - obs_ref[o].astype(F32))
        res_ref[o] = value.astype(BF16)
        flip_ref[o] = value.T.astype(BF16)


def backward_kernel(tab, tiles_ref, *refs):
    ins, outs, (acc, rays) = refs[: -1 - 2 * NX], refs[-1 - 2 * NX : -2], refs[-2:]
    own, (nz, _, edge) = ins[0].shape[0], outs[0].shape
    for n, ref in enumerate(ins):
        rays[n * own : (n + 1) * own] = ref[...]
    acc[...] = jnp.zeros_like(acc)

    def body(j, t, u, p, q):
        pair = jnp.concatenate([tiles_ref[t], tiles_ref[u]], axis=1)
        terms = jnp.dot(rays[tab[TAKE + j]], pair, preferred_element_type=F32)
        acc[p] += terms[:, :edge]
        acc[q] += terms[:, edge:]

    sweep(tab, body)
    outs[0][...] = acc[:nz].astype(BF16)
    for n, out in enumerate(outs[1:]):
        at = (NX - 1 - n // 2) * nz + n % 2 * (nz // 2)
        out[...] = acc[at : at + nz // 2].astype(BF16)


def add_kernel(*refs):
    for n in range(len(refs) // 3):
        refs[-2 + n][...] = (refs[2 * n][...].astype(F32) + refs[2 * n + 1][...].astype(F32)).astype(BF16)


def sum_kernel(here_ref, *refs):
    out, half = refs[-1], here_ref.shape[0] // 2
    for n in range(2):
        rows = slice(n * half, (n + 1) * half)
        total = here_ref[rows].astype(F32)
        for ref in refs[2 * n : 2 * n + 2]:
            total += ref[...].astype(F32)
        out[rows] = total.astype(BF16)


def update_kernel(step_size, grad_ref, cur_ref, new_ref, *copies):
    total = grad_ref[0].astype(F32)
    for k in range(1, grad_ref.shape[0]):
        total += grad_ref[k].astype(F32)
    new = jnp.maximum(cur_ref[...] - step_size * total.T, 0.0)
    new_ref[...] = new
    for copy in copies:
        value = new.astype(BF16)
        for k in range(copy.shape[0]):
            copy[k] = value


def call(kernel, shapes, specs, mib, scratch=(), outs=None, work=0):
    return pl.pallas_call(
        kernel,
        out_shape=tuple(jax.ShapeDtypeStruct(shape, dtype) for shape, dtype in shapes),
        in_specs=specs,
        out_specs=outs or (VMEM,) * len(shapes),
        scratch_shapes=list(scratch),
        compiler_params=pltpu.CompilerParams(vmem_limit_bytes=mib << 20),
        cost_estimate=pl.CostEstimate(flops=work, transcendentals=0, bytes_accessed=2 << 20),
    )


def shards(image, tiles, tile_slot, tile_block, slot_ray, sinogram, weights):
    n_space = lax.axis_size("space")
    n_angle = lax.axis_size("angle")
    nz, ny = n_angle // NX, n_space // CORES
    z_groups = [[z * NX + x for z in range(nz)] for x in range(NX)]
    tile_mats = tiles[0]
    own = sinogram.shape[1]
    edge = tile_mats.shape[1]
    slices = image.shape[1]
    blocks = image.shape[0] * n_angle // edge
    slots = slot_ray.shape[1]
    count = tile_slot.shape[1]
    step_size = 0.2 * math.sqrt(blocks / (n_angle * own))
    tile = (edge, slices)
    work = 2 * edge * edge * slices * count

    def along_x(value, d):
        return lax.ppermute(value, "angle", [(i, i // NX * NX + (i + d) % NX) for i in range(n_angle)])

    def along_y(value, d):
        return lax.ppermute(value, "space", [(i, (i + d * CORES) % n_space) for i in range(n_space)])

    def across(value):
        return lax.ppermute(value, "space", [(i, i ^ 1) for i in range(n_space)])

    def along_z(value):
        return lax.all_to_all(value, "angle", 0, 0, axis_index_groups=z_groups, tiled=True)

    def iterate(iteration, current, copies, table):
        column = along_z(copies)
        if table is None:
            sources = (tile_slot[0], tile_block[0], slot_ray[0], tile_mats)
            table = call(
                functools.partial(table_kernel, own, ny, nz),
                [((TABLE,), jnp.int32), ((count + 1, *tile_mats.shape[1:]), BF16)],
                [HBM] * 4,
                8,
                [pltpu.SMEM((size,), jnp.int32) for size in (count, count, slots)]
                + [pltpu.SemaphoreType.DMA((4,))],
                outs=(SMEM, VMEM),
                work=work,
            )(*[pltpu.with_memory_space_constraint(source, pltpu.HBM) for source in sources])
        columns = {d: along_x(column, d) for d in (RIGHT, LEFT, ACROSS)}
        columns[0] = column
        mine, other = call(
            forward_kernel,
            [((ny * own, *tile), BF16)] * 2,
            [SMEM] + [VMEM] * (1 + NX),
            12,
            [pltpu.VMEM((slots, *tile), F32), pltpu.VMEM((blocks, *tile), BF16)],
            work=work,
        )(*table, *[columns[d] for d in range(NX)])
        near, *far = call(
            functools.partial(merge_kernel, own),
            [((own, *tile), F32)] + [((own, *tile), BF16)] * (ny - 1),
            [VMEM] * 2,
            8,
        )(mine, across(other))
        residual, flipped = call(
            owner_kernel, [((own, *tile), BF16)] * 2, [VMEM] * (2 + ny), 8
        )(sinogram[0], weights[0], near, *[along_y(far[d - 1], d) for d in range(1, ny)])
        same = [flipped] + [along_y(flipped, d) for d in range(1, ny)]
        rays = same + [across(value) for value in same]

        half = ((nz // 2, *tile), BF16)
        here, right_low, right_high, far_low, far_high, left_low, left_high = call(
            backward_kernel,
            [((nz, *tile), BF16)] + [half] * (2 * NX - 2),
            [SMEM] + [VMEM] * (1 + len(rays)),
            12,
            [pltpu.VMEM((blocks, *tile), F32), pltpu.VMEM((n_space * own, *tile), BF16)],
            work=work,
        )(*table, *rays)
        from_left, from_right = along_x(far_low, RIGHT), along_x(far_high, LEFT)
        right_high, left_low = along_x(right_high, RIGHT), along_x(left_low, LEFT)
        right_low, left_high = call(add_kernel, [half] * 2, [VMEM] * 4, 8)(right_low, from_left, left_high, from_right)
        right_low, left_high = along_x(right_low, RIGHT), along_x(left_high, LEFT)
        (column,) = call(sum_kernel, [((nz, *tile), BF16)], [VMEM] * 5, 8)(
            here, right_low, left_low, right_high, left_high
        )
        terms = along_z(column)
        more = iteration + 1 < ITERS
        current, *rest = call(
            functools.partial(update_kernel, step_size), [(tile, F32)] + [((nz, *tile), BF16)] * more, [VMEM] * 2, 8
        )(terms, current)
        return (current, residual, rest[0] if more else None, table)

    current, table = image, None
    copies = jnp.broadcast_to(image.astype(BF16)[None], (nz, *tile))
    for iteration in range(ITERS):
        current, residual, copies, table = iterate(iteration, current, copies, table)
    return (current, residual[None])


def solution(mesh):
    placed = (
        P(("space", "angle"), None),
        P("space", "angle", None, None),
        P("space", "angle"),
        P("space", "angle"),
        P("space", "angle"),
        P("angle", "space", None, None),
        P("angle", "space", None, None),
    )
    return jax.shard_map(
        shards,
        mesh=mesh,
        in_specs=placed,
        out_specs=(P(("space", "angle"), None), P("angle", "space", None, None)),
        check_vma=False,
    )
```

```python
import functools
import math

import jax
import jax.numpy as jnp
from jax import lax
from jax.experimental import pallas as pl
from jax.experimental.pallas import tpu as pltpu
from jax.sharding import PartitionSpec as P

ITERS = 2
NX = 4
CORES = 2
UNROLL = 26
RIGHT, ACROSS, LEFT = 1, 2, 3

SMEM = pl.BlockSpec(memory_space=pltpu.SMEM)
VMEM = pl.BlockSpec(memory_space=pltpu.VMEM)
HBM = pl.BlockSpec(memory_space=pltpu.HBM)
BF16, F32 = jnp.bfloat16, jnp.float32

ROOM = 128
TILE, SEAT, SLOT, SEND, TAKE, STEPS, TABLE = 0, ROOM, 2 * ROOM, 320, 336, 352, 384


def table_kernel(own, ny, nz, *refs):
    sources, (tab, near_tiles), lists, sems = refs[:4], refs[4:6], refs[6:9], refs[9]
    slot_ref, block_ref, ray_ref = lists
    tiles, slots = slot_ref.shape[0], ray_ref.shape[0]
    targets = (*lists, near_tiles.at[pl.ds(0, tiles)])
    copies = [
        pltpu.make_async_copy(source, target, sems.at[n]) for n, (source, target) in enumerate(zip(sources, targets))
    ]
    for copy in copies:
        copy.start()
    near_tiles[tiles] = jnp.zeros_like(near_tiles[tiles])
    here, me = lax.axis_index("space"), lax.rem(lax.axis_index("angle"), NX)
    y, core = here // CORES, lax.rem(here, CORES)
    zero = jnp.int32(0)

    def clear(i, carry):
        for u in range(8):
            tab[TILE + i * 8 + u] = jnp.int32(tiles)
            tab[SEAT + i * 8 + u] = zero
        for u in range(4):
            tab[SLOT + i * 4 + u] = zero
        return carry

    lax.fori_loop(0, ROOM // 8, clear, 0)
    for copy in copies[:3]:
        copy.wait()

    def count(i, counts):
        for u in range(4):
            j = slot_ref[i * 4 + u]
            counts = tuple(c + (j == g).astype(jnp.int32) for g, c in enumerate(counts))
        return counts

    counts = lax.fori_loop(0, tiles // 4, count, (zero,) * slots)
    at = zero
    for j in range(slots):
        ray = ray_ref[j]
        owner = ray // own
        o = ray - owner * own
        theirs = owner // CORES
        side = jnp.where(lax.rem(owner, CORES) == core, 0, ny)
        tab[SEND + j] = (side + lax.rem(theirs - y + ny, ny)) * own + o
        tab[TAKE + j] = (side + lax.rem(y - theirs + ny, ny)) * own + o
        ray_ref[j] = at
        pairs = (counts[j] + 1) // 2

        def mark(i, carry, j=j, first=at // 2):
            tab[SLOT + first + i] = jnp.int32(j)
            return carry

        lax.fori_loop(0, pairs, mark, 0)
        at = at + 2 * pairs
    tab[STEPS] = (at + 2 * UNROLL - 1) // (2 * UNROLL)

    def place(i, carry):
        for u in range(4):
            t = i * 4 + u
            b, j = block_ref[t], slot_ref[t]
            seat = ray_ref[j]
            ray_ref[j] = seat + 1
            tab[TILE + seat] = t
            tab[SEAT + seat] = lax.rem(me - lax.rem(b, NX) + NX, NX) * nz + b // NX
        return carry

    lax.fori_loop(0, tiles // 4, place, 0)
    copies[3].wait()


def sweep(tab, body):
    def step(i, carry):
        for u in range(UNROLL):
            pair = i * UNROLL + u
            body(tab[SLOT + pair], *[tab[at + 2 * pair + n] for at in (TILE, SEAT) for n in (0, 1)])
        return carry

    lax.fori_loop(0, tab[STEPS], step, 0)


def forward_kernel(tab, tiles_ref, *refs):
    columns, (mine_ref, other_ref, acc, pix) = refs[:NX], refs[NX:]
    nz, half = columns[0].shape[0], mine_ref.shape[0]
    for d, column in enumerate(columns):
        pix[d * nz : (d + 1) * nz] = column[...]
    acc[...] = jnp.zeros_like(acc)
    for out in (mine_ref, other_ref):
        out[...] = jnp.zeros_like(out)

    def body(j, t, u, p, q):
        pair = jnp.concatenate([tiles_ref[t], tiles_ref[u]], axis=1)
        pixels = jnp.concatenate([pix[p], pix[q]], axis=0)
        acc[j] += jnp.dot(pair, pixels, preferred_element_type=F32)

    sweep(tab, body)
    for j in range(acc.shape[0]):
        seat = tab[SEND + j]

        @pl.when(seat < half)
        def _():
            mine_ref[seat] = acc[j].astype(BF16)

        @pl.when(seat >= half)
        def _():
            other_ref[seat - half] = acc[j].astype(BF16)


def merge_kernel(own, mine_ref, other_ref, near_ref, *far_refs):
    near_ref[...] = mine_ref[:own].astype(F32) + other_ref[:own].astype(F32)
    for d, ref in enumerate(far_refs, 1):
        rows = slice(d * own, (d + 1) * own)
        ref[...] = (mine_ref[rows].astype(F32) + other_ref[rows].astype(F32)).astype(BF16)


def owner_kernel(far_count, obs_ref, scale_ref, near_ref, *refs):
    far, flip_ref, res = refs[: far_count], refs[far_count], refs[far_count + 1 :]
    for o in range(obs_ref.shape[0]):
        total = near_ref[o]
        for ref in far:
            total += ref[o].astype(F32)
        value = scale_ref[o].astype(F32) * (total - obs_ref[o].astype(F32))
        for ref in res:
            ref[o] = value.astype(BF16)
        flip_ref[o] = value.T.astype(BF16)


def backward_kernel(tab, tiles_ref, *refs):
    ins, outs, (acc, rays) = refs[: -1 - 2 * NX], refs[-1 - 2 * NX : -2], refs[-2:]
    (nz, _, edge) = outs[0].shape
    at = 0
    for ref in ins:
        rays[at : at + ref.shape[0]] = ref[...]
        at += ref.shape[0]
    acc[...] = jnp.zeros_like(acc)

    def body(j, t, u, p, q):
        pair = jnp.concatenate([tiles_ref[t], tiles_ref[u]], axis=1)
        terms = jnp.dot(rays[tab[TAKE + j]], pair, preferred_element_type=F32)
        acc[p] += terms[:, :edge]
        acc[q] += terms[:, edge:]

    sweep(tab, body)
    outs[0][...] = acc[:nz].astype(BF16)
    for n, out in enumerate(outs[1:]):
        at = (NX - 1 - n // 2) * nz + n % 2 * (nz // 2)
        out[...] = acc[at : at + nz // 2].astype(BF16)


def add_kernel(*refs):
    for n in range(len(refs) // 3):
        refs[-2 + n][...] = (refs[2 * n][...].astype(F32) + refs[2 * n + 1][...].astype(F32)).astype(BF16)


def sum_kernel(here_ref, *refs):
    out, half = refs[-1], here_ref.shape[0] // 2
    for n in range(2):
        rows = slice(n * half, (n + 1) * half)
        total = here_ref[rows].astype(F32)
        for ref in refs[2 * n : 2 * n + 2]:
            total += ref[...].astype(F32)
        out[rows] = total.astype(BF16)


def update_kernel(step_size, grad_ref, cur_ref, new_ref, *copies):
    total = grad_ref[0].astype(F32)
    for k in range(1, grad_ref.shape[0]):
        total += grad_ref[k].astype(F32)
    new = jnp.maximum(cur_ref[...] - step_size * total.T, 0.0)
    new_ref[...] = new
    for copy in copies:
        value = new.astype(BF16)
        for k in range(copy.shape[0]):
            copy[k] = value


def call(kernel, shapes, specs, mib, scratch=(), outs=None, work=0):
    return pl.pallas_call(
        kernel,
        out_shape=tuple(jax.ShapeDtypeStruct(shape, dtype) for shape, dtype in shapes),
        in_specs=specs,
        out_specs=outs or (VMEM,) * len(shapes),
        scratch_shapes=list(scratch),
        compiler_params=pltpu.CompilerParams(vmem_limit_bytes=mib << 20),
        cost_estimate=pl.CostEstimate(flops=work, transcendentals=0, bytes_accessed=2 << 20),
    )


def shards(image, tiles, tile_slot, tile_block, slot_ray, sinogram, weights):
    n_space = lax.axis_size("space")
    n_angle = lax.axis_size("angle")
    nz, ny = n_angle // NX, n_space // CORES
    z_groups = [[z * NX + x for z in range(nz)] for x in range(NX)]
    tile_mats = tiles[0]
    own = sinogram.shape[1]
    edge = tile_mats.shape[1]
    slices = image.shape[1]
    blocks = image.shape[0] * n_angle // edge
    slots = slot_ray.shape[1]
    count = tile_slot.shape[1]
    step_size = 0.2 * math.sqrt(blocks / (n_angle * own))
    tile = (edge, slices)
    work = 2 * edge * edge * slices * count

    def along_x(value, d):
        return lax.ppermute(value, "angle", [(i, i // NX * NX + (i + d) % NX) for i in range(n_angle)])

    def along_y(value, d):
        return lax.ppermute(value, "space", [(i, (i + d * CORES) % n_space) for i in range(n_space)])

    def across(value):
        return lax.ppermute(value, "space", [(i, i ^ 1) for i in range(n_space)])

    def along_z(value):
        return lax.all_to_all(value, "angle", 0, 0, axis_index_groups=z_groups, tiled=True)

    def iterate(iteration, current, copies, table):
        column = along_z(copies)
        if table is None:
            sources = (tile_slot[0], tile_block[0], slot_ray[0], tile_mats)
            table = call(
                functools.partial(table_kernel, own, ny, nz),
                [((TABLE,), jnp.int32), ((count + 1, *tile_mats.shape[1:]), BF16)],
                [HBM] * 4,
                8,
                [pltpu.SMEM((size,), jnp.int32) for size in (count, count, slots)]
                + [pltpu.SemaphoreType.DMA((4,))],
                outs=(SMEM, VMEM),
                work=work,
            )(*[pltpu.with_memory_space_constraint(source, pltpu.HBM) for source in sources])
        columns = {d: along_x(column, d) for d in (ACROSS, RIGHT, LEFT)}
        columns[0] = column
        mine, other = call(
            forward_kernel,
            [((ny * own, *tile), BF16)] * 2,
            [SMEM] + [VMEM] * (1 + NX),
            12,
            [pltpu.VMEM((slots, *tile), F32), pltpu.VMEM((blocks, *tile), BF16)],
            work=work,
        )(*table, *[columns[d] for d in range(NX)])
        near, *far = call(
            functools.partial(merge_kernel, own),
            [((own, *tile), F32)] + [((own, *tile), BF16)] * (ny - 1),
            [VMEM] * 2,
            8,
        )(mine, across(other))
        more = iteration + 1 < ITERS
        flipped, *residual = call(
            functools.partial(owner_kernel, ny - 1), [((own, *tile), BF16)] * (1 + (not more)), [VMEM] * (2 + ny), 8
        )(sinogram[0], weights[0], near, *[along_y(far[d - 1], d) for d in range(1, ny)])
        same = [flipped] + [along_y(flipped, d) for d in range(1, ny)]
        rays = same + [across(same[0]), across(jnp.concatenate(same[1:]))]
        half = ((nz // 2, *tile), BF16)
        here, right_low, right_high, far_low, far_high, left_low, left_high = call(
            backward_kernel,
            [((nz, *tile), BF16)] + [half] * (2 * NX - 2),
            [SMEM] + [VMEM] * (1 + len(rays)),
            12,
            [pltpu.VMEM((blocks, *tile), F32), pltpu.VMEM((n_space * own, *tile), BF16)],
            work=work,
        )(*table, *rays)
        from_left, from_right = along_x(far_low, RIGHT), along_x(far_high, LEFT)
        right_high, left_low = along_x(right_high, RIGHT), along_x(left_low, LEFT)
        right_low, left_high = call(add_kernel, [half] * 2, [VMEM] * 4, 8)(right_low, from_left, left_high, from_right)
        right_low, left_high = along_x(right_low, RIGHT), along_x(left_high, LEFT)
        (column,) = call(sum_kernel, [((nz, *tile), BF16)], [VMEM] * 5, 8)(
            here, right_low, left_low, right_high, left_high
        )
        terms = along_z(column)
        current, *rest = call(
            functools.partial(update_kernel, step_size), [(tile, F32)] + [((nz, *tile), BF16)] * more, [VMEM] * 2, 8
        )(terms, current)
        return (current, residual, rest[0] if more else None, table)

    current, table = image, None
    copies = jnp.broadcast_to(image.astype(BF16)[None], (nz, *tile))
    for iteration in range(ITERS):
        current, residual, copies, table = iterate(iteration, current, copies, table)
    return (current, residual[0][None])


def solution(mesh):
    placed = (
        P(("space", "angle"), None),
        P("space", "angle", None, None),
        P("space", "angle"),
        P("space", "angle"),
        P("space", "angle"),
        P("angle", "space", None, None),
        P("angle", "space", None, None),
    )
    return jax.shard_map(
        shards,
        mesh=mesh,
        in_specs=placed,
        out_specs=(P(("space", "angle"), None), P("angle", "space", None, None)),
        check_vma=False,
    )
```
